32 devices in a mesh: blk: 8 (over y, x, core), grp: 4 (over z).
Axes of the slice: x: 2, y: 2, z: 4, core: 2. Of those that a mesh axis runs over, the one named last changes fastest.
Arguments:
- image_emb: bfloat16 [2048, 1152], P(('blk', 'grp')), may hold values from -0.5 to 0.5, as said below
- text_emb: bfloat16 [2048, 1152], P(('blk', 'grp')), may hold values from -0.5 to 0.5
- log_scale: float32 [1], replicated, may hold values from 2.8 to 3.2
- logit_bias: float32 [1], replicated, may hold values from -5.5 to -4.5
Outputs:
- image_grad: float32 [2048, 1152], P(('blk', 'grp'))
- text_grad: float32 [2048, 1152], P(('blk', 'grp'))
The draws below stay inside these ranges and needn't reach their ends.
Inputs may be any that keep to these rules, and one draw needn't show every extreme that they name: Entries of image_emb lie within the range; row j of text_emb is partly aligned with row j of image_emb.
All inputs are finite; a program needn't handle non-finite values.
Results may differ from the reference program's by a relative error of at most 0.0052.
Values may be sent and summed in bfloat16 or wider, within the bound.
No kernel may reach another device: no remote copies, remote signals or barrier semaphores. Data moves between devices by JAX's collectives and lax.ppermute only.
A program may use at most 64 MiB of HBM per device.

```python
import jax
import jax.numpy as jnp
from jax import lax

D = 1152
BATCH = 2048
N_BLK = 8


def paired_rows(key):
    keys = jax.random.split(jax.random.fold_in(key, 11), 2)
    shared = jax.random.normal(keys[0], (BATCH, D), jnp.float32)
    noise = jax.random.normal(keys[1], (BATCH, D), jnp.float32)
    image_rows = shared
    text_rows = 0.25 * shared + 0.97 * noise
    image_rows = jnp.clip(0.03 * image_rows, -0.5, 0.5)
    text_rows = jnp.clip(0.03 * text_rows, -0.5, 0.5)
    return (image_rows, text_rows)


def draw_image_emb(key, part):
    return paired_rows(key)[0].astype(jnp.bfloat16)


def draw_text_emb(key, part):
    return paired_rows(key)[1].astype(jnp.bfloat16)


def setup_inputs(seed: int = 0) -> dict:
    splits = jax.random.split(jax.random.key(seed), 5)
    image_emb = draw_image_emb(jax.random.fold_in(splits[4], 71), 0)
    text_emb = draw_text_emb(jax.random.fold_in(splits[4], 71), 0)
    log_scale = jnp.clip(jax.random.uniform(splits[2], (1,), jnp.float32, 2.8, 3.2), 2.8, 3.2)
    logit_bias = jnp.clip(jax.random.uniform(splits[3], (1,), jnp.float32, -5.5, -4.5), -5.5, -4.5)
    return dict(image_emb=image_emb, text_emb=text_emb, log_scale=log_scale, logit_bias=logit_bias)


def unit_rows(raw_rows):
    values = raw_rows.astype(jnp.float32)
    recip = lax.rsqrt(lax.optimization_barrier(jnp.sum(values * values, axis=1, keepdims=True)) + 1e-06)
    return (values * recip, recip)

def back_rows(exact, recip, upstream):
    along = lax.optimization_barrier(jnp.sum(exact * upstream, axis=1, keepdims=True))
    return recip * (upstream - exact * along)

def reference(image_emb, text_emb, log_scale, logit_bias):
    img_exact, img_recip = unit_rows(image_emb)
    txt_exact, txt_recip = unit_rows(text_emb)
    img_unit = img_exact.astype(jnp.bfloat16)
    txt_unit = txt_exact.astype(jnp.bfloat16)
    scale_value = jnp.exp(log_scale[0])
    shift_value = logit_bias[0]
    span_rows = BATCH // N_BLK
    img_index = jnp.arange(BATCH, dtype=jnp.int32)

    def one_block(grad_img, inputs):
        text_rows, first_row = inputs
        scores = jnp.dot(text_rows, img_unit.T, preferred_element_type=jnp.float32)
        logits = scale_value * scores + shift_value
        text_index = first_row + jnp.arange(span_rows, dtype=jnp.int32)
        match = (text_index[:, None] == img_index[None, :]).astype(jnp.float32)
        coef = (scale_value * (jax.nn.sigmoid(logits) - match)).astype(jnp.bfloat16)
        grad_txt = jnp.dot(coef, img_unit, preferred_element_type=jnp.float32)
        grad_img = grad_img + jnp.dot(coef.T, text_rows, preferred_element_type=jnp.float32)
        return (grad_img, grad_txt)
    firsts = jnp.arange(N_BLK, dtype=jnp.int32) * span_rows
    start_grad = jnp.zeros((BATCH, D), jnp.float32)
    unit_img_grad, unit_txt_grad = lax.scan(one_block, start_grad, (txt_unit.reshape(N_BLK, span_rows, D), firsts))
    unit_txt_grad = unit_txt_grad.reshape(BATCH, D)
    return (back_rows(img_exact, img_recip, unit_img_grad), back_rows(txt_exact, txt_recip, unit_txt_grad))
```

```python
import functools

import jax
import jax.numpy as jnp
from jax import lax
from jax.experimental import pallas as pl
from jax.experimental.pallas import tpu as pltpu
from jax.sharding import PartitionSpec as P


VMEM = pl.BlockSpec(memory_space=pltpu.VMEM)
SMEM = pl.BlockSpec(memory_space=pltpu.SMEM)


def partners(count, step):
    if count & (count - 1) == 0:
        return [(place, place ^ step) for place in range(count)]
    return [(place, (place + step) % count) for place in range(count)]


def moved(value, axis, pairs):
    return lax.ppermute(value, axis, pairs)


def sibling(value, count):
    return moved(value, "blk", [(place, place ^ 1) for place in range(count)])


def chip_step(value, count, step):
    pairs = [
        (2 * source + core, 2 * target + core)
        for source, target in partners(count // 2, step)
        for core in range(2)
    ]
    return moved(value, "blk", pairs)


def returned(pairs):
    return [(target, source) for source, target in pairs]


def unit_rows(raw):
    values = raw.astype(jnp.float32)
    recip = lax.rsqrt(jnp.sum(values * values, axis=1, keepdims=True) + 1e-06)
    return values * recip, recip


def back_rows(raw, upstream):
    exact, recip = unit_rows(raw)
    along = jnp.sum(exact * upstream, axis=1, keepdims=True)
    return recip * (upstream - exact * along)


def prepare_kernel(*refs):
    unit = refs[-1]
    rows = refs[0].shape[0]
    for place, raw in enumerate(refs[:-1]):
        unit[pl.ds(place * rows, rows), :] = unit_rows(raw[...])[0].astype(jnp.bfloat16)


def coef_rows(texts, images, log_scale, bias, diagonal):
    scale = jnp.exp(jnp.full((1, 1), log_scale[0], jnp.float32))
    scores = lax.dot_general(
        images, texts, (((1,), (1,)), ((), ())), preferred_element_type=jnp.float32
    )
    probs = jax.nn.sigmoid(scale * scores + bias[0])
    if diagonal:
        row = lax.broadcasted_iota(jnp.int32, probs.shape, 0)
        column = lax.broadcasted_iota(jnp.int32, probs.shape, 1)
        probs = probs - (row == column).astype(jnp.float32)
    return (scale * probs).astype(jnp.bfloat16)


def block_kernel(diagonal, log_scale, bias, texts, raw, coef, unit, grad):
    images = unit_rows(raw[...])[0].astype(jnp.bfloat16)
    unit[...] = images
    weights = coef_rows(texts[...], images, log_scale, bias, diagonal)
    coef[...] = weights
    grad[...] = jnp.dot(weights, texts[...], preferred_element_type=jnp.float32).astype(grad.dtype)


def text_kernel(first, rows, blocks, *refs):
    coefs, units, out = refs[:blocks], refs[blocks : 2 * blocks], refs[-1]
    weights = jnp.concatenate([ref[:, pl.ds(first, rows)] for ref in coefs], axis=0)
    images = jnp.concatenate([ref[...] for ref in units], axis=0)
    out[...] = lax.dot_general(
        weights, images, (((0,), (0,)), ((), ())), preferred_element_type=jnp.float32
    ).astype(out.dtype)


def join_kernel(rows, kept, got, own, *sent):
    own[...] = kept[pl.ds(0, rows), :] + got[pl.ds(0, rows), :].astype(jnp.float32)
    for place, ref in enumerate(sent):
        part = pl.ds((place + 1) * rows, rows)
        ref[...] = (kept[part, :] + got[part, :].astype(jnp.float32)).astype(ref.dtype)


def finish_kernel(raw, own, *refs):
    total = own[...]
    for ref in refs[:-1]:
        total = total + ref[...].astype(jnp.float32)
    refs[-1][...] = back_rows(raw[...], total)


def call(kernel, outs, scalars, *args):
    return pl.pallas_call(
        kernel,
        out_shape=outs,
        in_specs=[SMEM] * scalars + [VMEM] * (len(args) - scalars),
        out_specs=jax.tree.map(lambda _: VMEM, outs),
        compiler_params=pltpu.CompilerParams(vmem_limit_bytes=24 << 20),
    )(*args)


def local(image_emb, text_emb, log_scale, logit_bias):
    rows, width = image_emb.shape
    blk_count = lax.axis_size("blk")
    grp_count = lax.axis_size("grp")
    chips = blk_count // 2
    shape = jax.ShapeDtypeStruct

    grp_steps = list(range(1, grp_count))
    if grp_count == 4:
        grp_steps = [2, 3, 1]
    chip_steps = list(reversed(range(1, chips)))

    far_images = [moved(image_emb, "grp", partners(grp_count, step)) for step in grp_steps]
    same_core = [text_emb] + [chip_step(text_emb, blk_count, step) for step in chip_steps]
    other_core = [sibling(block, blk_count) for block in same_core]

    texts = call(
        prepare_kernel,
        shape((blk_count * rows, width), jnp.bfloat16),
        0,
        *same_core,
        *other_core,
    )

    coefs, units, grads = [], [], []
    for place, raw in enumerate([image_emb] + far_images):
        coef, unit, grad = call(
            functools.partial(block_kernel, place == 0),
            (
                shape((rows, blk_count * rows), jnp.bfloat16),
                shape((rows, width), jnp.bfloat16),
                shape((rows, width), jnp.float32 if place == 0 else jnp.bfloat16),
            ),
            2,
            log_scale,
            logit_bias,
            texts,
            raw,
        )
        coefs.append(coef)
        units.append(unit)
        grads.append(grad)
    image_parts = [
        moved(grad, "grp", returned(partners(grp_count, step)))
        for step, grad in zip(grp_steps, grads[1:])
    ]

    half = chips * rows
    for_sibling = call(
        functools.partial(text_kernel, half, half, grp_count),
        shape((half, width), jnp.bfloat16),
        0,
        *coefs,
        *units,
    )
    got = sibling(for_sibling, blk_count)
    kept = call(
        functools.partial(text_kernel, 0, half, grp_count),
        shape((half, width), jnp.float32),
        0,
        *coefs,
        *units,
    )
    own_text, *sent = call(
        functools.partial(join_kernel, rows),
        (shape((rows, width), jnp.float32),) + (shape((rows, width), jnp.bfloat16),) * (chips - 1),
        0,
        kept,
        got,
    )
    text_parts = []
    for step, part in zip(chip_steps, sent):
        pairs = [
            (2 * source + core, 2 * target + core)
            for source, target in returned(partners(chips, step))
            for core in range(2)
        ]
        text_parts.append(moved(part, "blk", pairs))

    out = shape((rows, width), jnp.float32)
    text_grad = call(finish_kernel, out, 0, text_emb, own_text, *text_parts)
    image_grad = call(finish_kernel, out, 0, image_emb, grads[0], *image_parts)
    return image_grad, text_grad


def solution(mesh):
    placed = (P(("blk", "grp"), None), P(("blk", "grp"), None), P(), P())
    return jax.shard_map(
        local,
        mesh=mesh,
        in_specs=placed,
        out_specs=(P(("blk", "grp"), None), P(("blk", "grp"), None)),
        check_vma=False,
    )
```
